32 devices in a mesh: blk: 16 (over z, y, x), pitch: 2 (over core).
Axes of the slice: x: 2, y: 2, z: 4, core: 2. Of those that a mesh axis runs over, the one named last changes fastest.
Arguments:
- psi_prev: float32 [6, 16, 128, 256], P(None, None, 'blk', 'pitch'), may hold values from -6 to 6
- forcing: float32 [6, 16, 128, 256], P(None, None, 'blk', 'pitch'), may hold values from -6 to 6
- kappa: float32 [16, 128, 256], P(None, 'blk', 'pitch'), may hold values from 1.5 to 3
- jac_local: float32 [6, 6, 16, 128, 256], P(None, None, None, 'blk', 'pitch'), may hold values from -0.5 to 0.5
- face_weight: float32 [4, 16, 128, 256], P(None, None, 'blk', 'pitch'), may hold values from 0.35 to 0.5
- flux_jac: float32 [4, 16, 6, 6], replicated, may hold values from -1.25 to 1.25
- face_map: int32 [16, 2, 128], P('blk', 'pitch'), may hold values from 0 to 127, each once within a row
- row_id: int32 [16], replicated, may hold values from 0 to 4, as said below
- blades: int32 [16], replicated, may hold values from 16 to 96
- harmonics: int32 [32], replicated, may hold values from 1 to 127
Outputs:
- psi_out: float32 [6, 16, 128, 256], P(None, None, 'blk', 'pitch')
The draws below stay inside these ranges and needn't reach their ends.
Inputs may be any that keep to these rules, and one draw needn't show every extreme that they name: row_id starts at 0 and rises by 0 or 1 from one block to the next, ending at exactly 4; it rises at block 9 and not at block 8.
All inputs are finite; a program needn't handle non-finite values.
Results may differ from the reference program's by a relative error of at most 0.0001.
Values sent between devices are 32-bit elements; how exact they have to be, the bound alone decides.
A program may use at most 64 MiB of HBM per device.

```python
import math
import jax
import jax.numpy as jnp
from jax import lax

NV = 6
NR = 16
AXD = 8
THD = 128
NH = 32
STEPS = 2
BLOCKS = 16
SECTORS = 2
NAX = 128
NTH = 256


def draw_row_id(key, part):
    position = jnp.arange(BLOCKS, dtype=jnp.int32)
    shuffled = jax.random.permutation(key, BLOCKS).astype(jnp.int32)
    excluded = (position == 0) | (position == BLOCKS // 2) | (position == BLOCKS // 2 + 1)
    scores = jnp.where(excluded, shuffled + BLOCKS, shuffled)
    order = jnp.argsort(scores, stable=True).astype(jnp.int32)
    chosen_count = BLOCKS // 4 - 1
    chosen = order[:chosen_count]
    picked = jnp.any(position[:, None] == chosen[None, :], axis=1)
    breaks = picked.astype(jnp.int32)
    breaks = jnp.where(position == BLOCKS // 2 + 1, 1, breaks)
    return jnp.cumsum(breaks).astype(jnp.int32)


def touch_ends(drawn, stream_key, least, high):
    place = [jax.random.randint(jax.random.fold_in(stream_key, axis), (), 0, length) for axis, length in enumerate(drawn.shape)]
    widest = drawn.shape.index(max(drawn.shape))
    beside = place[:widest] + [(place[widest] + 1) % drawn.shape[widest]] + place[widest + 1:]
    return drawn.at[tuple(place)].set(least).at[tuple(beside)].set(high)


def block_levels(stream_key, shape, pieces, smallest, top_value):
    level, own = 1.0, jax.random.fold_in(stream_key, 6)
    for axis_at, shards_of in pieces:
        steps = jnp.exp(jax.random.uniform(jax.random.fold_in(own, axis_at), (shards_of,), jnp.float32, smallest / len(pieces), top_value / len(pieces)))
        level = level * jnp.repeat(steps, shape[axis_at] // shards_of).reshape([-1 if axis == axis_at else 1 for axis in range(len(shape))])
    return level


def scatter_about(own_key, extent, width, bound, shards=(), kind=jnp.bfloat16):
    array = width * jax.random.normal(own_key, extent, jnp.float32)
    if shards:
        array = array * block_levels(own_key, extent, shards, -0.22, 0.18)
    return jnp.clip(array, -bound, bound).astype(kind)


def setup_inputs(seed: int = 0) -> dict:
    keys = jax.random.split(jax.random.key(seed), 11)
    return {
        "psi_prev": scatter_about(keys[0], (NV, NR, NAX, NTH), 1.0, 6.0, ((2, 16), (3, 2)), jnp.float32),
        "forcing": scatter_about(keys[1], (NV, NR, NAX, NTH), 1.0, 6.0, ((2, 16), (3, 2)), jnp.float32),
        "kappa": jnp.clip(jnp.exp(math.log(3.0) - 0.6931472 * jax.random.uniform(keys[2], (NR, NAX, NTH), jnp.float32) ** block_levels(keys[2], (NR, NAX, NTH), ((1, 16), (2, 2)), -0.2, 0.2)), 1.5, 3.0),
        "jac_local": scatter_about(keys[3], (NV, NV, NR, NAX, NTH), 0.08, 0.5, ((3, 16), (4, 2)), jnp.float32),
        "face_weight": jnp.clip(0.35 + 0.15 * jax.random.uniform(keys[4], (4, NR, NAX, NTH), jnp.float32) ** block_levels(keys[4], (4, NR, NAX, NTH), ((2, 16), (3, 2)), -0.2, 0.2), 0.35, 0.5),
        "flux_jac": scatter_about(keys[5], (4, NR, NV, NV), 0.4, 1.25, (), jnp.float32),
        "face_map": jax.vmap(lambda own: jax.random.permutation(own, THD))(jax.random.split(keys[6], BLOCKS * SECTORS)).reshape((BLOCKS, SECTORS, THD)).astype(jnp.int32),
        "row_id": draw_row_id(jax.random.fold_in(keys[10], 71), 0),
        "blades": touch_ends(jax.random.randint(keys[8], (BLOCKS,), 16, 97), jax.random.fold_in(keys[8], 1), 16, 96).astype(jnp.int32),
        "harmonics": touch_ends(jax.random.randint(keys[9], (NH,), 1, NTH // 2), jax.random.fold_in(keys[9], 1), 1, (NTH // 2) - 1).astype(jnp.int32),
    }


PRECISE = lax.Precision.HIGHEST
FULL_TURN = 2.0 * math.pi
SECTION_WEIGHTS = (0.25, 0.5, 1.0)


def contributions(adjoint, face_weight, flux_jac):
    projected = jnp.einsum("drji,jrxt->dirxt", flux_jac, adjoint, precision=PRECISE)
    return projected * face_weight[:, None]


def reference(psi_prev, forcing, kappa, jac_local, face_weight, flux_jac, face_map, row_id, blades, harmonics):
    num_vars = psi_prev.shape[0]
    num_bands = psi_prev.shape[1]
    sector_start = (jnp.arange(SECTORS, dtype=jnp.int32) * THD)[None, :, None]
    gather_index = (face_map + sector_start).reshape(BLOCKS, NTH).astype(jnp.int32)
    inverse = jnp.argsort(gather_index, axis=1).astype(jnp.int32)
    scatter_index = jnp.concatenate([inverse[1:], inverse[-1:]], axis=0)
    positions = jnp.arange(BLOCKS, dtype=jnp.int32)
    row_before = jnp.concatenate([row_id[:1], row_id[:-1]])
    row_after = jnp.concatenate([row_id[1:], row_id[-1:]])
    same_before = (positions > 0) & (row_before == row_id)
    has_after = positions < BLOCKS - 1
    same_after = has_after & (row_after == row_id)
    crossing_after = has_after & (row_after != row_id)
    blade_here = blades[row_id]
    blade_after = blades[row_after]
    theta_cells = jnp.arange(NTH, dtype=jnp.int32)
    products = (harmonics[:, None] * theta_cells[None, :]) % NTH
    angles = products.astype(jnp.float32) * (FULL_TURN / NTH)
    cosine_table = jnp.cos(angles)
    sine_table = jnp.sin(angles)
    lag_steps = (harmonics[None, :] * blade_after[:, None]) % blade_here[:, None]
    phase_lag = lag_steps.astype(jnp.float32) * FULL_TURN / blade_here[:, None].astype(jnp.float32)
    phase_cos = jnp.cos(phase_lag)[None, None]
    phase_sin = jnp.sin(phase_lag)[None, None]

    def apply_operator(adjoint):
        flows = contributions(adjoint, face_weight, flux_jac)
        blocked = flows.reshape(4, num_vars, num_bands, BLOCKS, AXD, NTH)
        toward_lo = blocked[0]
        toward_hi = blocked[1]
        last_faces = toward_hi[:, :, :, -1, :]
        before = jnp.concatenate([jnp.zeros_like(last_faces[:, :, :1]), last_faces[:, :, :-1]], axis=2)
        from_before = jnp.take_along_axis(before, gather_index[None, None], axis=3)
        from_before = jnp.where(same_before[None, None, :, None], from_before, 0.0)
        first_faces = toward_lo[:, :, :, 0, :]
        after = jnp.concatenate([first_faces[:, :, 1:], jnp.zeros_like(first_faces[:, :, :1])], axis=2)
        mapped_after = jnp.take_along_axis(after, scatter_index[None, None], axis=3)
        real_part = jnp.einsum("vrbt,kt->vrbk", after, cosine_table, precision=PRECISE)
        imag_part = -jnp.einsum("vrbt,kt->vrbk", after, sine_table, precision=PRECISE)
        turned_re = real_part * phase_cos + imag_part * phase_sin
        turned_im = imag_part * phase_cos - real_part * phase_sin
        rebuilt = jnp.einsum("vrbk,kt->vrbt", turned_re, cosine_table, precision=PRECISE)
        rebuilt = (rebuilt - jnp.einsum("vrbk,kt->vrbt", turned_im, sine_table, precision=PRECISE)) * (2.0 / NTH)
        from_after = jnp.where(same_after[None, None, :, None], mapped_after,
                               jnp.where(crossing_after[None, None, :, None], rebuilt, 0.0))
        incoming = jnp.concatenate([from_before[:, :, :, None, :], toward_hi[:, :, :, :-1, :]], axis=3)
        incoming = incoming + jnp.concatenate([toward_lo[:, :, :, 1:, :], from_after[:, :, :, None, :]], axis=3)
        incoming = incoming.reshape(num_vars, num_bands, NAX, NTH)
        incoming = incoming + jnp.roll(flows[3], 1, axis=3) + jnp.roll(flows[2], -1, axis=3)
        coupled = jnp.einsum("jirxt,jrxt->irxt", jac_local, adjoint, precision=PRECISE)
        return kappa * adjoint + coupled - incoming

    adjoint = psi_prev
    for step_index in range(STEPS):
        source = forcing + adjoint
        start_field = adjoint
        current = adjoint
        for section_weight in SECTION_WEIGHTS:
            current = start_field + section_weight * (source - apply_operator(current)) / kappa
        adjoint = current
    return adjoint
```

```python
import functools
import math

import jax
import jax.numpy as jnp
from jax import lax
from jax.experimental import pallas as pl
from jax.experimental.pallas import tpu as pltpu
from jax.sharding import PartitionSpec as P

STEPS = 2
SECTION_WEIGHTS = (0.25, 0.5, 1.0)
SWEEPS = STEPS * len(SECTION_WEIGHTS)
FULL_TURN = 2.0 * math.pi
HIGHEST = lax.Precision.HIGHEST
MESH = pl.DeviceIdType.MESH
F32 = jnp.float32


def dot(a, b):
    return jnp.dot(a, b, precision=HIGHEST, preferred_element_type=F32)


def exact_mod(value, modulus):
    rest = value - jnp.floor(value / modulus) * modulus
    rest = jnp.where(rest < 0.0, rest + modulus, rest)
    return jnp.where(rest >= modulus, rest - modulus, rest)


def kernel(
    n_blk, n_pit, n_v, n_r, ax, th, n_h,
    psi_h, forc_h, kap_h, jac_h, fw_h, flux, fm, hrow, rid, blades, harm,
    out,
    psi, forc, kap, jac, fw, cur, st, src, qinv, tang, lob, hib,
    fsend, lsend, msend, fmsend, frecv, lrecv, mrecv, fmrecv,
    umat, pmat, hcol, frow, wbig,
    in_sem, fs_sem, fr_sem, ls_sem, lr_sem, ms_sem, mr_sem, fms_sem, fmr_sem,
):
    b = lax.axis_index("blk")
    p = lax.axis_index("pitch")
    rows = n_v * n_r
    n_t = th * n_pit
    p_left = lax.rem(p + n_pit - 1, n_pit)
    p_right = lax.rem(p + 1, n_pit)
    has_lo = b > 0
    has_hi = b < n_blk - 1

    loads = [
        pltpu.make_async_copy(a, c, in_sem.at[i])
        for i, (a, c) in enumerate(
            ((psi_h, psi), (fw_h, fw), (forc_h, forc), (kap_h, kap), (jac_h, jac))
        )
    ]
    for load in loads:
        load.start()

    barrier = pltpu.get_barrier_semaphore()

    def greet(blk, pit):
        pl.semaphore_signal(
            barrier, inc=1, device_id={"blk": blk, "pitch": pit}, device_id_type=MESH
        )

    greet(b, p_right)
    if n_pit > 2:
        greet(b, p_left)

    @pl.when(has_lo)
    def _():
        for q in range(n_pit):
            greet(b - 1, jnp.int32(q))

    @pl.when(has_hi)
    def _():
        for q in range(n_pit):
            greet(b + 1, jnp.int32(q))

    def tile(a):
        return jnp.concatenate([a] * n_v, axis=0)

    def face_w(d, x):
        return tile(fw[pl.ds(d * n_r * ax + x, n_r, stride=ax), :])

    def f_copy(s, q_to, q_slot):
        return pltpu.make_async_remote_copy(
            src_ref=fsend.at[s], dst_ref=frecv.at[s, q_slot],
            send_sem=fs_sem.at[s, q_to], recv_sem=fr_sem.at[s, q_slot],
            device_id={"blk": b - 1, "pitch": jnp.int32(q_to)}, device_id_type=MESH,
        )

    def l_copy(s):
        return pltpu.make_async_remote_copy(
            src_ref=lsend.at[s], dst_ref=lrecv.at[s],
            send_sem=ls_sem.at[s], recv_sem=lr_sem.at[s],
            device_id={"blk": b + 1, "pitch": p}, device_id_type=MESH,
        )

    def fm_copy():
        return pltpu.make_async_remote_copy(
            src_ref=fmsend, dst_ref=fmrecv, send_sem=fms_sem, recv_sem=fmr_sem,
            device_id={"blk": b - 1, "pitch": p}, device_id_type=MESH,
        )

    if n_pit == 2:
        m_routes = ((p_right, 0),)
    else:
        m_routes = ((p_right, 0), (p_left, 1))

    def m_copy(s, target, slot):
        return pltpu.make_async_remote_copy(
            src_ref=msend.at[s], dst_ref=mrecv.at[s, slot],
            send_sem=ms_sem.at[s, slot], recv_sem=mr_sem.at[s, slot],
            device_id={"blk": b, "pitch": target}, device_id_type=MESH,
        )

    fmsend[...] = jnp.broadcast_to(fm[...].astype(F32), fmsend.shape)
    for k in range(n_h):
        hcol[pl.ds(k, 1), :] = jnp.full((1, th), harm[k], jnp.int32).astype(F32)
    for j in range(n_v):
        for i in range(n_v):
            frow[i, :, j * n_r : (j + 1) * n_r] = flux[j * n_v + i]
    row_at = lax.broadcasted_iota(jnp.int32, (n_r, rows), 0)
    col_at = lax.broadcasted_iota(jnp.int32, (n_r, rows), 1)
    same_band = lax.rem(col_at, n_r) == row_at
    for d in range(4):
        for i in range(n_v):
            wbig[pl.ds((d * n_v + i) * n_r, n_r), :] = jnp.where(
                same_band, frow[i, d : d + 1, :], 0.0
            )
    hib[0] = jnp.zeros((rows, th), F32)
    lob[ax] = jnp.zeros((rows, th), F32)

    loads[0].wait()
    loads[1].wait()

    def spread(x, carry):
        cur[0, x] = psi[pl.ds(x, rows, stride=ax), :]
        return carry

    lax.fori_loop(0, ax, spread, 0)

    sides = jnp.minimum(b, 1) + jnp.minimum(n_blk - 1 - b, 1)
    pl.semaphore_wait(barrier, len(m_routes) + n_pit * sides)

    @pl.when(has_lo)
    def _():
        fm_copy().start()

    lane = lax.broadcasted_iota(jnp.int32, (rows, th), 1)

    def build_maps():
        row_here = rid[b]
        row_before = rid[jnp.maximum(b - 1, 0)]
        row_after = rid[jnp.minimum(b + 1, n_blk - 1)]
        same_before = jnp.where(row_before == row_here, 1.0, 0.0).astype(F32)
        same_after = jnp.where(row_after == row_here, 1.0, 0.0).astype(F32)
        up_t = lax.broadcasted_iota(jnp.int32, (th, th), 0).astype(F32)
        pmat[...] = jnp.where(up_t == fmsend[0:1, :], same_before, 0.0)
        blade_here = blades[row_here].astype(F32)
        blade_after = blades[row_after].astype(F32)
        h = hcol[...]
        here = (lax.broadcasted_iota(jnp.int32, (n_h, th), 1) + p * th).astype(F32)
        bu = jnp.full((n_h, th), blade_here, F32)
        phase = exact_mod(h * blade_after, bu) * FULL_TURN / bu
        angle = exact_mod(h * here, jnp.full((n_h, th), float(n_t), F32)) * (FULL_TURN / n_t)
        cos_w, sin_w = jnp.cos(angle), jnp.sin(angle)
        cos_p, sin_p = jnp.cos(phase), jnp.sin(phase)
        scale = (1.0 - same_after) * (2.0 / n_t)
        c2 = (cos_w * cos_p + sin_w * sin_p) * scale
        s2 = (sin_w * cos_p - cos_w * sin_p) * scale
        hr = hrow[...].astype(F32)
        for q in range(n_pit):
            there = lax.broadcasted_iota(jnp.int32, (th, n_h), 0).astype(F32) + float(q * th)
            turn = exact_mod(hr * there, jnp.full((th, n_h), float(n_t), F32))
            turn = turn * (FULL_TURN / n_t)
            umat[pl.ds(q * th, th), :] = dot(jnp.cos(turn), c2) + dot(jnp.sin(turn), s2)

        @pl.when(has_hi)
        def _():
            fm_copy().wait_recv()
            mapped = jnp.where(up_t == fmrecv[0:1, :], same_after, 0.0).T
            own = pl.ds(pl.multiple_of(p * th, th), th)
            umat[own, :] = umat[own, :] + mapped

    for s in range(SWEEPS):
        k = s % len(SECTION_WEIGHTS)
        weight = SECTION_WEIGHTS[k]
        now, later = s % 2, (s + 1) % 2

        fsend[s] = dot(wbig[0:rows, :], cur[now, 0]) * face_w(0, 0)
        lsend[s] = dot(wbig[rows : 2 * rows, :], cur[now, ax - 1]) * face_w(1, ax - 1)

        @pl.when(has_lo)
        def _(s=s):
            for q in range(n_pit):
                f_copy(s, q, p).start()

        @pl.when(has_hi)
        def _(s=s):
            l_copy(s).start()

        def flows(x, edges, now=now):
            v = cur[now, x]
            flow = dot(wbig[...], v)
            lob[x] = flow[0:rows] * face_w(0, x)
            hib[x + 1] = flow[rows : 2 * rows] * face_w(1, x)
            left = flow[2 * rows : 3 * rows] * face_w(2, x)
            right = flow[3 * rows :] * face_w(3, x)
            tang[x] = jnp.where(lane == 0, 0.0, pltpu.roll(right, 1, 1)) + jnp.where(
                lane == th - 1, 0.0, pltpu.roll(left, th - 1, 1)
            )
            edges = jnp.where(lane == x, right[:, th - 1 :], edges)
            return jnp.where(lane == ax + x, left[:, 0:1], edges)

        msend[s] = lax.fori_loop(0, ax, flows, jnp.zeros((rows, th), F32))
        for target, slot in m_routes:
            m_copy(s, target, slot).start()

        if s == 0:
            for load in loads[2:]:
                load.wait()

            def invert(x, carry):
                qinv[x] = 1.0 / kap[pl.ds(x, n_r, stride=ax), :]
                return carry

            lax.fori_loop(0, ax, invert, 0)

        def update(x, carry, now=now, later=later, k=k, weight=weight):
            v = cur[now, x]
            if k == 0:
                source = forc[pl.ds(x, rows, stride=ax), :] + v
                src[x] = source
                st[x] = v
                begin = v
            else:
                source = src[x]
                begin = st[x]
            total = source + tang[x] + hib[x] + lob[x + 1]
            total = total - tile(kap[pl.ds(x, n_r, stride=ax), :]) * v
            for j in range(n_v):
                coupling = jac[pl.ds(j * rows * ax + x, rows, stride=ax), :]
                total = total - coupling * tile(v[j * n_r : (j + 1) * n_r])
            cur[later, x] = begin + (weight * tile(qinv[x])) * total
            return carry

        lax.fori_loop(0, ax, update, 0)
        if s == 0:
            build_maps()

        for target, slot in m_routes:
            m_copy(s, target, slot).wait_recv()
        from_left = mrecv[s, 0]
        from_right = mrecv[s, len(m_routes) - 1]
        for x in range(ax):
            edge = jnp.where(lane == 0, from_left[:, x : x + 1], 0.0)
            edge = jnp.where(lane == th - 1, from_right[:, ax + x : ax + x + 1], edge)
            cur[later, x] = cur[later, x] + (weight * tile(qinv[x])) * edge

        @pl.when(has_lo)
        def _(s=s, later=later, weight=weight):
            l_copy(s).wait_recv()
            add = dot(lrecv[s], pmat[...])
            cur[later, 0] = cur[later, 0] + (weight * tile(qinv[0])) * add

        @pl.when(has_hi)
        def _(s=s, later=later, weight=weight):
            for q in range(n_pit):
                f_copy(s, q, q).wait_recv()
            add = dot(frecv[s, 0], umat[0:th, :])
            for q in range(1, n_pit):
                add = add + dot(frecv[s, q], umat[q * th : (q + 1) * th, :])
            cur[later, ax - 1] = cur[later, ax - 1] + (weight * tile(qinv[ax - 1])) * add

    def gather(x, carry):
        out[pl.ds(x, rows, stride=ax), :] = cur[SWEEPS % 2, x]
        return carry

    lax.fori_loop(0, ax, gather, 0)

    for s in range(SWEEPS):
        for target, slot in m_routes:
            m_copy(s, target, slot).wait_send()

        @pl.when(has_lo)
        def _(s=s):
            for q in range(n_pit):
                f_copy(s, q, p).wait_send()

        @pl.when(has_hi)
        def _(s=s):
            l_copy(s).wait_send()

    @pl.when(has_lo)
    def _():
        fm_copy().wait_send()


def per_device(
    n_blk, n_pit,
    psi_prev, forcing, kappa, jac_local, face_weight, flux_jac, face_map, row_id, blades, harmonics,
):
    n_v, n_r, ax, th = psi_prev.shape
    n_h = harmonics.shape[0]
    rows = n_v * n_r
    hbm = pl.BlockSpec(memory_space=pltpu.HBM)
    vmem = pl.BlockSpec(memory_space=pltpu.VMEM)
    smem = pl.BlockSpec(memory_space=pltpu.SMEM)
    field = (ax, rows, th)
    m_slots = 1 if n_pit == 2 else 2
    dma = pltpu.SemaphoreType.DMA
    result = pl.pallas_call(
        functools.partial(kernel, n_blk, n_pit, n_v, n_r, ax, th, n_h),
        out_shape=jax.ShapeDtypeStruct((rows * ax, th), F32),
        in_specs=[hbm] * 5 + [vmem] * 3 + [smem] * 3,
        out_specs=vmem,
        scratch_shapes=[
            pltpu.VMEM((rows * ax, th), F32),
            pltpu.VMEM((rows * ax, th), F32),
            pltpu.VMEM((n_r * ax, th), F32),
            pltpu.VMEM((n_v * rows * ax, th), F32),
            pltpu.VMEM((4 * n_r * ax, th), F32),
            pltpu.VMEM((2,) + field, F32),
            pltpu.VMEM(field, F32),
            pltpu.VMEM(field, F32),
            pltpu.VMEM((ax, n_r, th), F32),
            pltpu.VMEM(field, F32),
            pltpu.VMEM((ax + 1, rows, th), F32),
            pltpu.VMEM((ax + 1, rows, th), F32),
            pltpu.VMEM((SWEEPS, rows, th), F32),
            pltpu.VMEM((SWEEPS, rows, th), F32),
            pltpu.VMEM((SWEEPS, rows, th), F32),
            pltpu.VMEM((8, th), F32),
            pltpu.VMEM((SWEEPS, n_pit, rows, th), F32),
            pltpu.VMEM((SWEEPS, rows, th), F32),
            pltpu.VMEM((SWEEPS, m_slots, rows, th), F32),
            pltpu.VMEM((8, th), F32),
            pltpu.VMEM((n_pit * th, th), F32),
            pltpu.VMEM((th, th), F32),
            pltpu.VMEM((n_h, th), F32),
            pltpu.VMEM((n_v, 4, rows), F32),
            pltpu.VMEM((4 * rows, rows), F32),
            dma((5,)),
            dma((SWEEPS, n_pit)),
            dma((SWEEPS, n_pit)),
            dma((SWEEPS,)),
            dma((SWEEPS,)),
            dma((SWEEPS, m_slots)),
            dma((SWEEPS, m_slots)),
            dma(()),
            dma(()),
        ],
        compiler_params=pltpu.CompilerParams(
            collective_id=0, has_side_effects=True, vmem_limit_bytes=48 * 1024 * 1024
        ),
        name="adjoint_sections",
    )(
        psi_prev.reshape(rows * ax, th),
        forcing.reshape(rows * ax, th),
        kappa.reshape(n_r * ax, th),
        jac_local.reshape(n_v * rows * ax, th),
        face_weight.reshape(4 * n_r * ax, th),
        flux_jac.transpose(2, 3, 0, 1).reshape(n_v * n_v, 4, n_r),
        face_map.reshape(1, th),
        harmonics.reshape(1, n_h),
        row_id,
        blades,
        harmonics,
    )
    return result.reshape(n_v, n_r, ax, th)


def solution(mesh):
    return jax.shard_map(
        functools.partial(per_device, mesh.shape["blk"], mesh.shape["pitch"]),
        mesh=mesh,
        in_specs=(
            P(None, None, "blk", "pitch"),
            P(None, None, "blk", "pitch"),
            P(None, "blk", "pitch"),
            P(None, None, None, "blk", "pitch"),
            P(None, None, "blk", "pitch"),
            P(),
            P("blk", "pitch", None),
            P(),
            P(),
            P(),
        ),
        out_specs=P(None, None, "blk", "pitch"),
        check_vma=False,
    )
```

```python
import functools
import math

import jax
import jax.numpy as jnp
from jax import lax
from jax.experimental import pallas as pl
from jax.experimental.pallas import tpu as pltpu
from jax.sharding import PartitionSpec as P

STEPS = 2
SECTION_WEIGHTS = (0.25, 0.5, 1.0)
SWEEPS = STEPS * len(SECTION_WEIGHTS)
FULL_TURN = 2.0 * math.pi
HIGHEST = lax.Precision.HIGHEST
MESH = pl.DeviceIdType.MESH
F32 = jnp.float32


def dot(a, b):
    return jnp.dot(a, b, precision=HIGHEST, preferred_element_type=F32)


def exact_mod(value, modulus):
    rest = value - jnp.floor(value / modulus) * modulus
    rest = jnp.where(rest < 0.0, rest + modulus, rest)
    return jnp.where(rest >= modulus, rest - modulus, rest)


def kernel(
    n_blk, n_pit, n_v, n_r, ax, th, n_h,
    psi_h, forc_h, kap_h, jac_h, fw_h, flux, fm, hrow, rid, blades, harm,
    out,
    psi, forc, kap, jac, fw, cur, st, src, qinv, tang, lob, hib,
    fsend, lsend, msend, fmsend, frecv, lrecv, mrecv, fmrecv,
    umat, pmat, hcol, frow, wbig,
    in_sem, fs_sem, fr_sem, ls_sem, lr_sem, ms_sem, mr_sem, fms_sem, fmr_sem,
):
    b = lax.axis_index("blk")
    p = lax.axis_index("pitch")
    rows = n_v * n_r
    n_t = th * n_pit
    p_left = lax.rem(p + n_pit - 1, n_pit)
    p_right = lax.rem(p + 1, n_pit)
    has_lo = b > 0
    has_hi = b < n_blk - 1

    loads = [
        pltpu.make_async_copy(a, c, in_sem.at[i])
        for i, (a, c) in enumerate(
            ((psi_h, psi), (fw_h, fw), (forc_h, forc), (kap_h, kap), (jac_h, jac))
        )
    ]
    for load in loads:
        load.start()

    barrier = pltpu.get_barrier_semaphore()

    def greet(blk, pit):
        pl.semaphore_signal(
            barrier, inc=1, device_id={"blk": blk, "pitch": pit}, device_id_type=MESH
        )

    greet(b, p_right)
    if n_pit > 2:
        greet(b, p_left)

    @pl.when(has_lo)
    def _():
        for q in range(n_pit):
            greet(b - 1, jnp.int32(q))

    @pl.when(has_hi)
    def _():
        for q in range(n_pit):
            greet(b + 1, jnp.int32(q))

    def tile(a):
        return jnp.concatenate([a] * n_v, axis=0)

    def face_w(d, x):
        return tile(fw[pl.ds(d * n_r * ax + x, n_r, stride=ax), :])

    def f_copy(s, q_to, q_slot):
        return pltpu.make_async_remote_copy(
            src_ref=fsend.at[s], dst_ref=frecv.at[s, q_slot],
            send_sem=fs_sem.at[s, q_to], recv_sem=fr_sem.at[s, q_slot],
            device_id={"blk": b - 1, "pitch": jnp.int32(q_to)}, device_id_type=MESH,
        )

    def l_copy(s):
        return pltpu.make_async_remote_copy(
            src_ref=lsend.at[s], dst_ref=lrecv.at[s],
            send_sem=ls_sem.at[s], recv_sem=lr_sem.at[s],
            device_id={"blk": b + 1, "pitch": p}, device_id_type=MESH,
        )

    def fm_copy():
        return pltpu.make_async_remote_copy(
            src_ref=fmsend, dst_ref=fmrecv, send_sem=fms_sem, recv_sem=fmr_sem,
            device_id={"blk": b - 1, "pitch": p}, device_id_type=MESH,
        )

    if n_pit == 2:
        m_routes = ((p_right, 0),)
    else:
        m_routes = ((p_right, 0), (p_left, 1))

    def m_copy(s, target, slot):
        return pltpu.make_async_remote_copy(
            src_ref=msend.at[s], dst_ref=mrecv.at[s, slot],
            send_sem=ms_sem.at[s, slot], recv_sem=mr_sem.at[s, slot],
            device_id={"blk": b, "pitch": target}, device_id_type=MESH,
        )

    fmsend[...] = jnp.broadcast_to(fm[...].astype(F32), fmsend.shape)
    for k in range(n_h):
        hcol[pl.ds(k, 1), :] = jnp.full((1, th), harm[k], jnp.int32).astype(F32)
    for j in range(n_v):
        for i in range(n_v):
            frow[i, :, j * n_r : (j + 1) * n_r] = flux[j * n_v + i]
    row_at = lax.broadcasted_iota(jnp.int32, (n_r, rows), 0)
    col_at = lax.broadcasted_iota(jnp.int32, (n_r, rows), 1)
    same_band = lax.rem(col_at, n_r) == row_at
    for d in range(4):
        for i in range(n_v):
            wbig[pl.ds((d * n_v + i) * n_r, n_r), :] = jnp.where(
                same_band, frow[i, d : d + 1, :], 0.0
            )
    hib[0] = jnp.zeros((rows, th), F32)
    lob[ax] = jnp.zeros((rows, th), F32)

    loads[0].wait()
    loads[1].wait()

    def spread(x, carry):
        cur[0, x] = psi[pl.ds(x, rows, stride=ax), :]
        return carry

    lax.fori_loop(0, ax, spread, 0)

    sides = jnp.minimum(b, 1) + jnp.minimum(n_blk - 1 - b, 1)
    pl.semaphore_wait(barrier, len(m_routes) + n_pit * sides)

    @pl.when(has_lo)
    def _():
        fm_copy().start()

    lane = lax.broadcasted_iota(jnp.int32, (rows, th), 1)

    def build_maps():
        row_here = rid[b]
        row_before = rid[jnp.maximum(b - 1, 0)]
        row_after = rid[jnp.minimum(b + 1, n_blk - 1)]
        same_before = jnp.where(row_before == row_here, 1.0, 0.0).astype(F32)
        same_after = jnp.where(row_after == row_here, 1.0, 0.0).astype(F32)
        up_t = lax.broadcasted_iota(jnp.int32, (th, th), 0).astype(F32)
        pmat[...] = jnp.where(up_t == fmsend[0:1, :], same_before, 0.0)
        blade_here = blades[row_here].astype(F32)
        blade_after = blades[row_after].astype(F32)
        h = hcol[...]
        here = (lax.broadcasted_iota(jnp.int32, (n_h, th), 1) + p * th).astype(F32)
        bu = jnp.full((n_h, th), blade_here, F32)
        phase = exact_mod(h * blade_after, bu) * FULL_TURN / bu
        angle = exact_mod(h * here, jnp.full((n_h, th), float(n_t), F32)) * (FULL_TURN / n_t)
        cos_w, sin_w = jnp.cos(angle), jnp.sin(angle)
        cos_p, sin_p = jnp.cos(phase), jnp.sin(phase)
        scale = (1.0 - same_after) * (2.0 / n_t)
        c2 = (cos_w * cos_p + sin_w * sin_p) * scale
        s2 = (sin_w * cos_p - cos_w * sin_p) * scale
        hr = hrow[...].astype(F32)
        for q in range(n_pit):
            there = lax.broadcasted_iota(jnp.int32, (th, n_h), 0).astype(F32) + float(q * th)
            turn = exact_mod(hr * there, jnp.full((th, n_h), float(n_t), F32))
            turn = turn * (FULL_TURN / n_t)
            umat[pl.ds(q * th, th), :] = dot(jnp.cos(turn), c2) + dot(jnp.sin(turn), s2)

        @pl.when(has_hi)
        def _():
            fm_copy().wait_recv()
            mapped = jnp.where(up_t == fmrecv[0:1, :], same_after, 0.0).T
            own = pl.ds(pl.multiple_of(p * th, th), th)
            umat[own, :] = umat[own, :] + mapped

    for s in range(SWEEPS):
        k = s % len(SECTION_WEIGHTS)
        weight = SECTION_WEIGHTS[k]
        now, later = s % 2, (s + 1) % 2

        fsend[s] = dot(wbig[0:rows, :], cur[now, 0]) * face_w(0, 0)
        lsend[s] = dot(wbig[rows : 2 * rows, :], cur[now, ax - 1]) * face_w(1, ax - 1)

        @pl.when(has_lo)
        def _(s=s):
            for q in range(n_pit):
                f_copy(s, q, p).start()

        @pl.when(has_hi)
        def _(s=s):
            l_copy(s).start()

        def flows(x, edges, now=now):
            v = cur[now, x]
            flow = dot(wbig[...], v)
            lob[x] = flow[0:rows] * face_w(0, x)
            hib[x + 1] = flow[rows : 2 * rows] * face_w(1, x)
            left = flow[2 * rows : 3 * rows] * face_w(2, x)
            right = flow[3 * rows :] * face_w(3, x)
            tang[x] = jnp.where(lane == 0, 0.0, pltpu.roll(right, 1, 1)) + jnp.where(
                lane == th - 1, 0.0, pltpu.roll(left, th - 1, 1)
            )
            edges = jnp.where(lane == x, right[:, th - 1 :], edges)
            return jnp.where(lane == ax + x, left[:, 0:1], edges)

        msend[s] = lax.fori_loop(0, ax, flows, jnp.zeros((rows, th), F32))
        for target, slot in m_routes:
            m_copy(s, target, slot).start()

        if s == 0:
            for load in loads[2:]:
                load.wait()

            def invert(x, carry):
                qinv[x] = 1.0 / kap[pl.ds(x, n_r, stride=ax), :]
                return carry

            lax.fori_loop(0, ax, invert, 0)

        def update(x, carry, now=now, later=later, k=k, weight=weight):
            v = cur[now, x]
            if k == 0:
                source = forc[pl.ds(x, rows, stride=ax), :] + v
                src[x] = source
                st[x] = v
                begin = v
            else:
                source = src[x]
                begin = st[x]
            total = source + tang[x] + hib[x] + lob[x + 1]
            total = total - tile(kap[pl.ds(x, n_r, stride=ax), :]) * v
            for j in range(n_v):
                coupling = jac[pl.ds(j * rows * ax + x, rows, stride=ax), :]
                total = total - coupling * tile(v[j * n_r : (j + 1) * n_r])
            cur[later, x] = begin + (weight * tile(qinv[x])) * total
            return carry

        lax.fori_loop(0, ax, update, 0)
        if s == 0:
            build_maps()

        for target, slot in m_routes:
            m_copy(s, target, slot).wait_recv()
        from_left = mrecv[s, 0]
        from_right = mrecv[s, len(m_routes) - 1]
        for x in range(ax):
            edge = jnp.where(lane == 0, from_left[:, x : x + 1], 0.0)
            edge = jnp.where(lane == th - 1, from_right[:, ax + x : ax + x + 1], edge)
            cur[later, x] = cur[later, x] + (weight * tile(qinv[x])) * edge

        @pl.when(has_lo)
        def _(s=s, later=later, weight=weight):
            l_copy(s).wait_recv()
            add = dot(lrecv[s], pmat[...])
            cur[later, 0] = cur[later, 0] + (weight * tile(qinv[0])) * add

        @pl.when(has_hi)
        def _(s=s, later=later, weight=weight):
            for q in range(n_pit):
                f_copy(s, q, q).wait_recv()
            add = dot(frecv[s, 0], umat[0:th, :])
            for q in range(1, n_pit):
                add = add + dot(frecv[s, q], umat[q * th : (q + 1) * th, :])
            cur[later, ax - 1] = cur[later, ax - 1] + (weight * tile(qinv[ax - 1])) * add

    def gather(x, carry):
        out[pl.ds(x, rows, stride=ax), :] = cur[SWEEPS % 2, x]
        return carry

    lax.fori_loop(0, ax, gather, 0)

    for s in range(SWEEPS):
        for target, slot in m_routes:
            m_copy(s, target, slot).wait_send()

        @pl.when(has_lo)
        def _(s=s):
            for q in range(n_pit):
                f_copy(s, q, p).wait_send()

        @pl.when(has_hi)
        def _(s=s):
            l_copy(s).wait_send()

    @pl.when(has_lo)
    def _():
        fm_copy().wait_send()


def per_device(
    n_blk, n_pit,
    psi_prev, forcing, kappa, jac_local, face_weight, flux_jac, face_map, row_id, blades, harmonics,
):
    n_v, n_r, ax, th = psi_prev.shape
    n_h = harmonics.shape[0]
    rows = n_v * n_r
    hbm = pl.BlockSpec(memory_space=pltpu.HBM)
    vmem = pl.BlockSpec(memory_space=pltpu.VMEM)
    smem = pl.BlockSpec(memory_space=pltpu.SMEM)
    field = (ax, rows, th)
    m_slots = 1 if n_pit == 2 else 2
    dma = pltpu.SemaphoreType.DMA
    result = pl.pallas_call(
        functools.partial(kernel, n_blk, n_pit, n_v, n_r, ax, th, n_h),
        out_shape=jax.ShapeDtypeStruct((rows * ax, th), F32),
        in_specs=[hbm] * 5 + [vmem] * 3 + [smem] * 3,
        out_specs=vmem,
        scratch_shapes=[
            pltpu.VMEM((rows * ax, th), F32),
            pltpu.VMEM((rows * ax, th), F32),
            pltpu.VMEM((n_r * ax, th), F32),
            pltpu.VMEM((n_v * rows * ax, th), F32),
            pltpu.VMEM((4 * n_r * ax, th), F32),
            pltpu.VMEM((2,) + field, F32),
            pltpu.VMEM(field, F32),
            pltpu.VMEM(field, F32),
            pltpu.VMEM((ax, n_r, th), F32),
            pltpu.VMEM(field, F32),
            pltpu.VMEM((ax + 1, rows, th), F32),
            pltpu.VMEM((ax + 1, rows, th), F32),
            pltpu.VMEM((SWEEPS, rows, th), F32),
            pltpu.VMEM((SWEEPS, rows, th), F32),
            pltpu.VMEM((SWEEPS, rows, th), F32),
            pltpu.VMEM((8, th), F32),
            pltpu.VMEM((SWEEPS, n_pit, rows, th), F32),
            pltpu.VMEM((SWEEPS, rows, th), F32),
            pltpu.VMEM((SWEEPS, m_slots, rows, th), F32),
            pltpu.VMEM((8, th), F32),
            pltpu.VMEM((n_pit * th, th), F32),
            pltpu.VMEM((th, th), F32),
            pltpu.VMEM((n_h, th), F32),
            pltpu.VMEM((n_v, 4, rows), F32),
            pltpu.VMEM((4 * rows, rows), F32),
            dma((5,)),
            dma((SWEEPS, n_pit)),
            dma((SWEEPS, n_pit)),
            dma((SWEEPS,)),
            dma((SWEEPS,)),
            dma((SWEEPS, m_slots)),
            dma((SWEEPS, m_slots)),
            dma(()),
            dma(()),
        ],
        compiler_params=pltpu.CompilerParams(
            collective_id=0, has_side_effects=True, vmem_limit_bytes=67043328
        ),
        name="adjoint_sections",
    )(
        psi_prev.reshape(rows * ax, th),
        forcing.reshape(rows * ax, th),
        kappa.reshape(n_r * ax, th),
        jac_local.reshape(n_v * rows * ax, th),
        face_weight.reshape(4 * n_r * ax, th),
        flux_jac.transpose(2, 3, 0, 1).reshape(n_v * n_v, 4, n_r),
        face_map.reshape(1, th),
        harmonics.reshape(1, n_h),
        row_id,
        blades,
        harmonics,
    )
    return result.reshape(n_v, n_r, ax, th)


def solution(mesh):
    return jax.shard_map(
        functools.partial(per_device, mesh.shape["blk"], mesh.shape["pitch"]),
        mesh=mesh,
        in_specs=(
            P(None, None, "blk", "pitch"),
            P(None, None, "blk", "pitch"),
            P(None, "blk", "pitch"),
            P(None, None, None, "blk", "pitch"),
            P(None, None, "blk", "pitch"),
            P(),
            P("blk", "pitch", None),
            P(),
            P(),
            P(),
        ),
        out_specs=P(None, None, "blk", "pitch"),
        check_vma=False,
    )
```

```python
import functools
import math

import jax
import jax.numpy as jnp
from jax import lax
from jax.experimental import pallas as pl
from jax.experimental.pallas import tpu as pltpu
from jax.sharding import PartitionSpec as P

STEPS = 2
SECTION_WEIGHTS = (0.25, 0.5, 1.0)
SWEEPS = STEPS * len(SECTION_WEIGHTS)
FULL_TURN = 2.0 * math.pi
HIGHEST = lax.Precision.HIGHEST
MESH = pl.DeviceIdType.MESH
F32 = jnp.float32


def dot(a, b):
    return jnp.dot(a, b, precision=HIGHEST, preferred_element_type=F32)


def narrow_dot(a, b):
    return jnp.dot(a, b, preferred_element_type=F32)


def split(a):
    high = a.astype(jnp.bfloat16)
    return high, (a - high.astype(F32)).astype(jnp.bfloat16)


def exact_mod(value, modulus):
    rest = value - jnp.floor(value / modulus) * modulus
    rest = jnp.where(rest < 0.0, rest + modulus, rest)
    return jnp.where(rest >= modulus, rest - modulus, rest)


def kernel(
    n_blk, n_pit, n_v, n_r, ax, th, n_h,
    psi_h, forc_h, kap_h, jac_h, fw_h, flux, fm, hrow, rid, blades, harm,
    out,
    psi, forc, kap, jac, fw, cur, st, src, qinv, tang, lob, hib,
    fsend, lsend, msend, fmsend, frecv, lrecv, mrecv, fmrecv,
    umat, pmat, hcol, frow, wbig, wcat, pmat2, uhigh, ulow,
    in_sem, fs_sem, fr_sem, ls_sem, lr_sem, ms_sem, mr_sem, fms_sem, fmr_sem,
):
    b = lax.axis_index("blk")
    p = lax.axis_index("pitch")
    rows = n_v * n_r
    n_t = th * n_pit
    p_left = lax.rem(p + n_pit - 1, n_pit)
    p_right = lax.rem(p + 1, n_pit)
    has_lo = b > 0
    has_hi = b < n_blk - 1

    loads = [
        pltpu.make_async_copy(a, c, in_sem.at[i])
        for i, (a, c) in enumerate(
            ((psi_h, psi), (fw_h, fw), (forc_h, forc), (kap_h, kap), (jac_h, jac))
        )
    ]
    for load in loads:
        load.start()

    barrier = pltpu.get_barrier_semaphore()

    def greet(blk, pit):
        pl.semaphore_signal(
            barrier, inc=1, device_id={"blk": blk, "pitch": pit}, device_id_type=MESH
        )

    greet(b, p_right)
    if n_pit > 2:
        greet(b, p_left)

    @pl.when(has_lo)
    def _():
        for q in range(n_pit):
            greet(b - 1, jnp.int32(q))

    @pl.when(has_hi)
    def _():
        for q in range(n_pit):
            greet(b + 1, jnp.int32(q))

    def tile(a):
        return jnp.concatenate([a] * n_v, axis=0)

    def face_w(d, x):
        return tile(fw[pl.ds(d * n_r * ax + x, n_r, stride=ax), :])

    def f_copy(s, q_to, q_slot):
        return pltpu.make_async_remote_copy(
            src_ref=fsend.at[s], dst_ref=frecv.at[s, q_slot],
            send_sem=fs_sem.at[s, q_to], recv_sem=fr_sem.at[s, q_slot],
            device_id={"blk": b - 1, "pitch": jnp.int32(q_to)}, device_id_type=MESH,
        )

    def l_copy(s):
        return pltpu.make_async_remote_copy(
            src_ref=lsend.at[s], dst_ref=lrecv.at[s],
            send_sem=ls_sem.at[s], recv_sem=lr_sem.at[s],
            device_id={"blk": b + 1, "pitch": p}, device_id_type=MESH,
        )

    def fm_copy():
        return pltpu.make_async_remote_copy(
            src_ref=fmsend, dst_ref=fmrecv, send_sem=fms_sem, recv_sem=fmr_sem,
            device_id={"blk": b - 1, "pitch": p}, device_id_type=MESH,
        )

    if n_pit == 2:
        m_routes = ((p_right, 0),)
    else:
        m_routes = ((p_right, 0), (p_left, 1))

    def m_copy(s, target, slot):
        return pltpu.make_async_remote_copy(
            src_ref=msend.at[s], dst_ref=mrecv.at[s, slot],
            send_sem=ms_sem.at[s, slot], recv_sem=mr_sem.at[s, slot],
            device_id={"blk": b, "pitch": target}, device_id_type=MESH,
        )

    fmsend[...] = jnp.broadcast_to(fm[...].astype(F32), fmsend.shape)
    for k in range(n_h):
        hcol[pl.ds(k, 1), :] = jnp.full((1, th), harm[k], jnp.int32).astype(F32)
    for j in range(n_v):
        for i in range(n_v):
            frow[i, :, j * n_r : (j + 1) * n_r] = flux[j * n_v + i]
    row_at = lax.broadcasted_iota(jnp.int32, (n_r, rows), 0)
    col_at = lax.broadcasted_iota(jnp.int32, (n_r, rows), 1)
    same_band = lax.rem(col_at, n_r) == row_at
    for d in range(4):
        for i in range(n_v):
            part = jnp.where(same_band, frow[i, d : d + 1, :], 0.0)
            high = part.astype(jnp.bfloat16).astype(F32)
            wbig[pl.ds((d * n_v + i) * n_r, n_r), 0:rows] = high
            wbig[pl.ds((d * n_v + i) * n_r, n_r), rows:] = part - high
    wcat[...] = wbig[...].astype(jnp.bfloat16)
    hib[0] = jnp.zeros((rows, th), F32)
    lob[ax] = jnp.zeros((rows, th), F32)

    loads[0].wait()
    loads[1].wait()

    def spread(x, carry):
        cur[0, x] = psi[pl.ds(x, rows, stride=ax), :]
        return carry

    lax.fori_loop(0, ax, spread, 0)

    sides = jnp.minimum(b, 1) + jnp.minimum(n_blk - 1 - b, 1)
    pl.semaphore_wait(barrier, len(m_routes) + n_pit * sides)

    @pl.when(has_lo)
    def _():
        fm_copy().start()

    def project(low_row, high_row, v):
        high, low = split(v)
        twice = jnp.concatenate([high, high], axis=0)
        return narrow_dot(wcat[low_row:high_row, :], twice) + narrow_dot(
            wcat[low_row:high_row, 0:rows], low
        )

    lane = lax.broadcasted_iota(jnp.int32, (rows, th), 1)

    def build_maps():
        row_here = rid[b]
        row_before = rid[jnp.maximum(b - 1, 0)]
        row_after = rid[jnp.minimum(b + 1, n_blk - 1)]
        same_before = jnp.where(row_before == row_here, 1.0, 0.0).astype(F32)
        same_after = jnp.where(row_after == row_here, 1.0, 0.0).astype(F32)
        up_t = lax.broadcasted_iota(jnp.int32, (th, th), 0).astype(F32)
        pmat[...] = jnp.where(up_t == fmsend[0:1, :], same_before, 0.0)
        blade_here = blades[row_here].astype(F32)
        blade_after = blades[row_after].astype(F32)
        h = hcol[...]
        here = (lax.broadcasted_iota(jnp.int32, (n_h, th), 1) + p * th).astype(F32)
        bu = jnp.full((n_h, th), blade_here, F32)
        phase = exact_mod(h * blade_after, bu) * FULL_TURN / bu
        angle = exact_mod(h * here, jnp.full((n_h, th), float(n_t), F32)) * (FULL_TURN / n_t)
        cos_w, sin_w = jnp.cos(angle), jnp.sin(angle)
        cos_p, sin_p = jnp.cos(phase), jnp.sin(phase)
        scale = (1.0 - same_after) * (2.0 / n_t)
        c2 = (cos_w * cos_p + sin_w * sin_p) * scale
        s2 = (sin_w * cos_p - cos_w * sin_p) * scale
        hr = hrow[...].astype(F32)
        for q in range(n_pit):
            there = lax.broadcasted_iota(jnp.int32, (th, n_h), 0).astype(F32) + float(q * th)
            turn = exact_mod(hr * there, jnp.full((th, n_h), float(n_t), F32))
            turn = turn * (FULL_TURN / n_t)
            umat[pl.ds(q * th, th), :] = dot(jnp.cos(turn), c2) + dot(jnp.sin(turn), s2)

        @pl.when(has_hi)
        def _():
            fm_copy().wait_recv()
            mapped = jnp.where(up_t == fmrecv[0:1, :], same_after, 0.0).T
            own = pl.ds(pl.multiple_of(p * th, th), th)
            umat[own, :] = umat[own, :] + mapped

        pmat2[0:th, :] = pmat[...].astype(jnp.bfloat16)
        pmat2[th:, :] = pmat[...].astype(jnp.bfloat16)
        for q in range(n_pit):
            high, low = split(umat[q * th : (q + 1) * th, :])
            uhigh[2 * q * th : (2 * q + 1) * th, :] = high
            uhigh[(2 * q + 1) * th : (2 * q + 2) * th, :] = high
            ulow[q * th : (q + 1) * th, :] = low

    for s in range(SWEEPS):
        k = s % len(SECTION_WEIGHTS)
        weight = SECTION_WEIGHTS[k]
        now, later = s % 2, (s + 1) % 2

        fsend[s] = project(0, rows, cur[now, 0]) * face_w(0, 0)
        lsend[s] = project(rows, 2 * rows, cur[now, ax - 1]) * face_w(1, ax - 1)

        @pl.when(has_lo)
        def _(s=s):
            for q in range(n_pit):
                f_copy(s, q, p).start()

        @pl.when(has_hi)
        def _(s=s):
            l_copy(s).start()

        def flows(pair, edges, now=now):
            both = jnp.concatenate([cur[now, 2 * pair], cur[now, 2 * pair + 1]], axis=1)
            flow2 = project(0, 4 * rows, both)
            for at in range(2):
                x = 2 * pair + at
                flow = flow2[:, at * th : (at + 1) * th]
                lob[x] = flow[0:rows] * face_w(0, x)
                hib[x + 1] = flow[rows : 2 * rows] * face_w(1, x)
                left = flow[2 * rows : 3 * rows] * face_w(2, x)
                right = flow[3 * rows :] * face_w(3, x)
                right = pltpu.roll(right, 1, 1)
                left = pltpu.roll(left, th - 1, 1)
                tang[x] = jnp.where(lane == 0, 0.0, right) + jnp.where(lane == th - 1, 0.0, left)
                msend[s, x] = jnp.where(lane == 0, right, left)
            return edges

        lax.fori_loop(0, ax // 2, flows, 0, unroll=True)
        for target, slot in m_routes:
            m_copy(s, target, slot).start()

        if s == 0:
            for load in loads[2:]:
                load.wait()

            def invert(x, carry):
                qinv[x] = 1.0 / kap[pl.ds(x, n_r, stride=ax), :]
                return carry

            lax.fori_loop(0, ax, invert, 0)

        def update(x, carry, now=now, later=later, k=k, weight=weight):
            v = cur[now, x]
            if k == 0:
                source = forc[pl.ds(x, rows, stride=ax), :] + v
                src[x] = source
                st[x] = v
                begin = v
            else:
                source = src[x]
                begin = st[x]
            total = source + tang[x] + hib[x] + lob[x + 1]
            total = total - tile(kap[pl.ds(x, n_r, stride=ax), :]) * v
            for j in range(n_v):
                coupling = jac[pl.ds(j * rows * ax + x, rows, stride=ax), :]
                total = total - coupling * tile(v[j * n_r : (j + 1) * n_r])
            cur[later, x] = begin + (weight * tile(qinv[x])) * total
            return carry

        lax.fori_loop(0, ax, update, 0, unroll=True)
        if s == 0:
            build_maps()

        for target, slot in m_routes:
            m_copy(s, target, slot).wait_recv()
        for x in range(ax):
            edge = jnp.where(lane == 0, mrecv[s, 0, x], 0.0)
            edge = jnp.where(lane == th - 1, mrecv[s, len(m_routes) - 1, x], edge)
            cur[later, x] = cur[later, x] + (weight * tile(qinv[x])) * edge

        @pl.when(has_lo)
        def _(s=s, later=later, weight=weight):
            l_copy(s).wait_recv()
            add = narrow_dot(jnp.concatenate(split(lrecv[s]), axis=1), pmat2[...])
            cur[later, 0] = cur[later, 0] + (weight * tile(qinv[0])) * add

        @pl.when(has_hi)
        def _(s=s, later=later, weight=weight):
            for q in range(n_pit):
                f_copy(s, q, q).wait_recv()
            add = jnp.zeros((rows, th), F32)
            for q in range(n_pit):
                high, low = split(frecv[s, q])
                add = add + narrow_dot(
                    jnp.concatenate([high, low], axis=1), uhigh[2 * q * th : (2 * q + 2) * th, :]
                )
                add = add + narrow_dot(high, ulow[q * th : (q + 1) * th, :])
            cur[later, ax - 1] = cur[later, ax - 1] + (weight * tile(qinv[ax - 1])) * add

    def gather(x, carry):
        out[pl.ds(x, rows, stride=ax), :] = cur[SWEEPS % 2, x]
        return carry

    lax.fori_loop(0, ax, gather, 0)

    for s in range(SWEEPS):
        for target, slot in m_routes:
            m_copy(s, target, slot).wait_send()

        @pl.when(has_lo)
        def _(s=s):
            for q in range(n_pit):
                f_copy(s, q, p).wait_send()

        @pl.when(has_hi)
        def _(s=s):
            l_copy(s).wait_send()

    @pl.when(has_lo)
    def _():
        fm_copy().wait_send()


def per_device(
    n_blk, n_pit,
    psi_prev, forcing, kappa, jac_local, face_weight, flux_jac, face_map, row_id, blades, harmonics,
):
    n_v, n_r, ax, th = psi_prev.shape
    n_h = harmonics.shape[0]
    rows = n_v * n_r
    hbm = pl.BlockSpec(memory_space=pltpu.HBM)
    vmem = pl.BlockSpec(memory_space=pltpu.VMEM)
    smem = pl.BlockSpec(memory_space=pltpu.SMEM)
    field = (ax, rows, th)
    m_slots = 1 if n_pit == 2 else 2
    dma = pltpu.SemaphoreType.DMA
    result = pl.pallas_call(
        functools.partial(kernel, n_blk, n_pit, n_v, n_r, ax, th, n_h),
        out_shape=jax.ShapeDtypeStruct((rows * ax, th), F32),
        in_specs=[hbm] * 5 + [vmem] * 3 + [smem] * 3,
        out_specs=vmem,
        scratch_shapes=[
            pltpu.VMEM((rows * ax, th), F32),
            pltpu.VMEM((rows * ax, th), F32),
            pltpu.VMEM((n_r * ax, th), F32),
            pltpu.VMEM((n_v * rows * ax, th), F32),
            pltpu.VMEM((4 * n_r * ax, th), F32),
            pltpu.VMEM((2,) + field, F32),
            pltpu.VMEM(field, F32),
            pltpu.VMEM(field, F32),
            pltpu.VMEM((ax, n_r, th), F32),
            pltpu.VMEM(field, F32),
            pltpu.VMEM((ax + 1, rows, th), F32),
            pltpu.VMEM((ax + 1, rows, th), F32),
            pltpu.VMEM((SWEEPS, rows, th), F32),
            pltpu.VMEM((SWEEPS, rows, th), F32),
            pltpu.VMEM((SWEEPS,) + field, F32),
            pltpu.VMEM((8, th), F32),
            pltpu.VMEM((SWEEPS, n_pit, rows, th), F32),
            pltpu.VMEM((SWEEPS, rows, th), F32),
            pltpu.VMEM((SWEEPS, m_slots) + field, F32),
            pltpu.VMEM((8, th), F32),
            pltpu.VMEM((n_pit * th, th), F32),
            pltpu.VMEM((th, th), F32),
            pltpu.VMEM((n_h, th), F32),
            pltpu.VMEM((n_v, 4, rows), F32),
            pltpu.VMEM((4 * rows, 2 * rows), F32),
            pltpu.VMEM((4 * rows, 2 * rows), jnp.bfloat16),
            pltpu.VMEM((2 * th, th), jnp.bfloat16),
            pltpu.VMEM((2 * n_pit * th, th), jnp.bfloat16),
            pltpu.VMEM((n_pit * th, th), jnp.bfloat16),
            dma((5,)),
            dma((SWEEPS, n_pit)),
            dma((SWEEPS, n_pit)),
            dma((SWEEPS,)),
            dma((SWEEPS,)),
            dma((SWEEPS, m_slots)),
            dma((SWEEPS, m_slots)),
            dma(()),
            dma(()),
        ],
        compiler_params=pltpu.CompilerParams(
            collective_id=0, has_side_effects=True, vmem_limit_bytes=67043328
        ),
        name="adjoint_sections",
    )(
        psi_prev.reshape(rows * ax, th),
        forcing.reshape(rows * ax, th),
        kappa.reshape(n_r * ax, th),
        jac_local.reshape(n_v * rows * ax, th),
        face_weight.reshape(4 * n_r * ax, th),
        flux_jac.transpose(2, 3, 0, 1).reshape(n_v * n_v, 4, n_r),
        face_map.reshape(1, th),
        harmonics.reshape(1, n_h),
        row_id,
        blades,
        harmonics,
    )
    return result.reshape(n_v, n_r, ax, th)


def solution(mesh):
    return jax.shard_map(
        functools.partial(per_device, mesh.shape["blk"], mesh.shape["pitch"]),
        mesh=mesh,
        in_specs=(
            P(None, None, "blk", "pitch"),
            P(None, None, "blk", "pitch"),
            P(None, "blk", "pitch"),
            P(None, None, None, "blk", "pitch"),
            P(None, None, "blk", "pitch"),
            P(),
            P("blk", "pitch", None),
            P(),
            P(),
            P(),
        ),
        out_specs=P(None, None, "blk", "pitch"),
        check_vma=False,
    )
```
